32 devices in a mesh: replica: 8 (over y, x, core), tensor: 4 (over z).
Axes of the slice: x: 2, y: 2, z: 4, core: 2. Of those that a mesh axis runs over, the one named last changes fastest.
Arguments:
- queries: bfloat16 [8, 512, 2560], P('replica', None, 'tensor'), may hold values from -160 to 160
- key_rows: bfloat16 [8, 512, 2560], P('replica', None, 'tensor'), may hold values from -4 to 4
- value_rows: bfloat16 [8, 512, 2560], P('replica', None, 'tensor'), may hold values from -6 to 6
- out_grads: bfloat16 [8, 512, 1024], P('replica', 'tensor'), may hold values from -6 to 6
- inner_weights: bfloat16 [8, 20, 128, 1024], P('replica', 'tensor'), may hold values from -0.15625 to 0.15625
- adam_first: bfloat16 [8, 20, 128, 1024], P('replica', 'tensor'), may hold values from -12 to 12
- adam_second: bfloat16 [8, 20, 128, 1024], P('replica', 'tensor'), may hold values from 1 to 16
- anchor: bfloat16 [20, 128, 1024], P('tensor'), may hold values from -0.125 to 0.125
- momentum: float32 [20, 128, 1024], P('tensor', 'replica'), may hold values from -0.06 to 0.06
Outputs:
- query_grads: bfloat16 [8, 512, 2560], P('replica', None, 'tensor')
- key_grads: bfloat16 [8, 512, 2560], P('replica', None, 'tensor')
- value_grads: bfloat16 [8, 512, 2560], P('replica', None, 'tensor')
- new_first: bfloat16 [8, 20, 128, 1024], P('replica', 'tensor')
- new_second: bfloat16 [8, 20, 128, 1024], P('replica', 'tensor')
- new_anchor: bfloat16 [20, 128, 1024], P('tensor')
- new_momentum: float32 [20, 128, 1024], P('tensor', 'replica')
The draws below stay inside these ranges and needn't reach their ends.
All inputs are finite; a program needn't handle non-finite values.
Results may differ from the reference program's by a relative error of at most 0.028.
Values may be sent and summed in bfloat16 or wider, within the bound.
A program may use at most 64 MiB of HBM per device.

```python
import math
import jax
import jax.numpy as jnp
from jax import lax

D = 1024
DH = 128
LEN = 512
WORKERS = 8
HEADS = 20
INNER = 2560


def drawn_pair(key):
    base = jax.random.fold_in(key, 11)
    query_key, row_key = jax.random.split(base, 2)
    shape = (WORKERS, HEADS, LEN, DH)
    query_heads = jnp.clip(jax.random.normal(query_key, shape, jnp.float32), -6.0, 6.0)
    key_heads = jnp.clip(jax.random.normal(row_key, shape, jnp.float32), -4.0, 4.0)
    return (query_heads, key_heads)


def widened(head_array):
    return jnp.transpose(head_array, (0, 2, 1, 3)).reshape(WORKERS, LEN, HEADS * DH).astype(jnp.bfloat16)


def draw_queries(key, part):
    return widened(drawn_pair(key)[0])


def draw_key_rows(key, part):
    return widened(drawn_pair(key)[1])


def strengthened(entries, stream_key, source, target, blocks, factor):
    def block_of(dim):
        return (jnp.arange(entries.shape[dim]) // (entries.shape[dim] // blocks)).reshape((-1,) + (1,) * (entries.ndim - 1 - dim))

    first = jax.random.permutation(stream_key, blocks)[block_of(target)]
    second = (block_of(target) + blocks // 2) % blocks
    return jnp.where((block_of(source) == first) | (block_of(source) == second), factor * entries, entries)


def levels(own_key, dims, shards, smallest, top_value):
    def one(axis_at, blocks):
        steps = jax.random.uniform(jax.random.fold_in(jax.random.fold_in(own_key, 6), axis_at), (blocks,), jnp.float32, smallest / len(shards), top_value / len(shards))
        return jnp.repeat(jnp.exp(steps), dims[axis_at] // blocks).reshape((-1,) + (1,) * (len(dims) - axis_at - 1))

    factor_of = one(*shards[0])
    for cut in shards[1:]:
        factor_of = factor_of * one(*cut)
    return factor_of


def gaussian(key, shape, scale, reach, cuts=(), held_as=jnp.bfloat16):
    drawn = jax.random.normal(key, shape, jnp.float32) * scale
    if len(cuts) > 0:
        drawn = levels(key, shape, cuts, -0.22, 0.18) * drawn
    return jnp.clip(drawn, min=-reach, max=reach).astype(held_as)


def bell_draw_with(rng, extent, deviation, limit, cuts, heavy, held_as=jnp.bfloat16):
    values = deviation * jax.random.normal(rng, extent, jnp.float32)
    if cuts:
        values = values * levels(rng, extent, cuts, -0.22, 0.18)
    return jnp.clip(strengthened(values, jax.random.fold_in(rng, 3), *heavy), -limit, limit).astype(held_as)


def setup_inputs(seed: int = 0) -> dict:
    key_list = jax.random.split(jax.random.key(seed), 10)
    queries = draw_queries(jax.random.fold_in(key_list[9], 71), 0)
    key_rows = draw_key_rows(jax.random.fold_in(key_list[9], 71), 0)
    value_rows = gaussian(key_list[2], (WORKERS, LEN, INNER), 1.0, 6.0, ((0, 8), (2, 4)))
    out_grads = gaussian(key_list[3], (WORKERS, LEN, D), 1.0, 6.0, ((0, 8), (1, 4)))
    inner_weights = bell_draw_with(key_list[4], (WORKERS, HEADS, DH, D), INNER ** -0.5, 0.15625, ((0, 8), (1, 4)), (0, 2, 8, 2.0))
    adam_first = gaussian(key_list[5], (WORKERS, HEADS, DH, D), 2.0, 12.0, ((0, 8), (1, 4)))
    adam_second = jnp.clip(jnp.exp(math.log(16.0) - 2.7725887 * jax.random.uniform(key_list[6], (WORKERS, HEADS, DH, D), jnp.float32) ** levels(key_list[6], (WORKERS, HEADS, DH, D), ((0, 8), (1, 4)), -0.2, 0.2)), 1.0, 16.0).astype(jnp.bfloat16)
    anchor = gaussian(key_list[7], (HEADS, DH, D), INNER ** -0.5, 0.125, ((0, 4),))
    momentum = gaussian(key_list[8], (HEADS, DH, D), 0.01, 0.06, ((0, 4), (1, 8)), jnp.float32)
    return dict(queries=queries, key_rows=key_rows, value_rows=value_rows, out_grads=out_grads, inner_weights=inner_weights, adam_first=adam_first, adam_second=adam_second, anchor=anchor, momentum=momentum)


beta_first = 0.9
beta_second = 0.95
correct_first = 0.9999734386011124
correct_second = 0.994079470779666
inner_rate = 0.01
decay_rate = 0.1
epsilon = 1e-08
outer_rate = 0.7
outer_beta = 0.9
highest = lax.Precision.HIGHEST

def lowered(values):
    return lax.optimization_barrier(values.astype(jnp.bfloat16)).astype(jnp.float32)

def worker_step(queries, key_rows, value_rows, out_grads, inner_weights, adam_first, adam_second, anchor_wide):
    score_scale = 1.0 / math.sqrt(DH)
    query_heads = queries.astype(jnp.float32).reshape(LEN, HEADS, DH)
    key_heads = key_rows.astype(jnp.float32).reshape(LEN, HEADS, DH)
    value_heads = value_rows.astype(jnp.float32).reshape(LEN, HEADS, DH)
    grads_out = out_grads.astype(jnp.float32)
    previous = inner_weights.astype(jnp.float32)
    scores = jnp.einsum('qhc,khc->hqk', query_heads, key_heads, precision=highest) * score_scale
    probs = jax.nn.softmax(scores, axis=-1)
    probs_low = lowered(probs)
    attention = lowered(jnp.einsum('hqk,khc->qhc', probs_low, value_heads, precision=highest))
    grad_proj = jnp.einsum('qhc,qd->hcd', attention, grads_out, precision=highest)
    grad_attn = lowered(jnp.einsum('qd,hcd->qhc', grads_out, previous, precision=highest))
    value_grads = jnp.einsum('hqk,qhc->khc', probs_low, grad_attn, precision=highest).astype(jnp.bfloat16)
    grad_probs = jnp.einsum('qhc,khc->hqk', grad_attn, value_heads, precision=highest)
    row_dot = jnp.einsum('qhc,qhc->hq', grad_attn, attention, precision=highest)
    grad_scores = lowered(probs * (grad_probs - row_dot[:, :, None]))
    query_grads = (jnp.einsum('hqk,khc->qhc', grad_scores, key_heads, precision=highest) * score_scale).astype(jnp.bfloat16)
    key_grads = (jnp.einsum('hqk,qhc->khc', grad_scores, query_heads, precision=highest) * score_scale).astype(jnp.bfloat16)
    first_moment = beta_first * adam_first.astype(jnp.float32) + (1.0 - beta_first) * grad_proj
    second_moment = beta_second * adam_second.astype(jnp.float32) + (1.0 - beta_second) * grad_proj * grad_proj
    stepped = previous - inner_rate * (first_moment / correct_first / (jnp.sqrt(second_moment / correct_second) + epsilon) + decay_rate * previous)
    delta_terms = (anchor_wide - stepped).astype(jnp.bfloat16)
    return (query_grads.reshape(LEN, INNER), key_grads.reshape(LEN, INNER), value_grads.reshape(LEN, INNER), first_moment.astype(jnp.bfloat16), second_moment.astype(jnp.bfloat16), delta_terms)

def reference(queries, key_rows, value_rows, out_grads, inner_weights, adam_first, adam_second, anchor, momentum):
    anchor_wide = anchor.astype(jnp.float32)

    def visit(summed, inputs):
        results = worker_step(*inputs, anchor_wide)
        deltas = lax.optimization_barrier(results[5]).astype(jnp.float32)
        return (summed + deltas, results[:5])
    summed, stacked = lax.scan(visit, jnp.zeros((HEADS, DH, D), jnp.float32), (queries, key_rows, value_rows, out_grads, inner_weights, adam_first, adam_second))
    average = summed / WORKERS
    new_momentum = outer_beta * momentum + average
    new_anchor = (anchor_wide - outer_rate * (average + outer_beta * new_momentum)).astype(jnp.bfloat16)
    return (stacked[0], stacked[1], stacked[2], stacked[3], stacked[4], new_anchor, new_momentum)
```

```python
import functools
import math

import jax
import jax.numpy as jnp
from jax import lax
from jax.experimental import pallas as pl
from jax.experimental.pallas import tpu as pltpu
from jax.sharding import PartitionSpec as P

DH = 128
CHUNKS = 8
DIRECT = 1
AHEAD = 5
SKEW = 3
SUM_LAG = 3
SPREAD_LAG = 3
UNROLL = 5
MID = 2
VMEM_BYTES = 67043328
SPARE = 2**17
MESH = pl.DeviceIdType.MESH

beta_first = 0.9
beta_second = 0.95
correct_first = 0.9999734386011124
correct_second = 0.994079470779666
inner_rate = 0.01
decay_rate = 0.1
epsilon = 1e-08
outer_rate = 0.7
outer_beta = 0.9

F32 = jnp.float32
BF16 = jnp.bfloat16


def dot(a, b, ca, cb):
    return lax.dot_general(a, b, (((ca,), (cb,)), ((), ())), preferred_element_type=F32)


def kernel(
    tensors,
    workers,
    q_hbm, k_hbm, v_hbm, g_hbm, w_hbm, m1_hbm, m2_hbm, anchor_hbm, mom_hbm,
    dq, dk, dv, n1, n2, na, nm,
    q, k, v, g, w, m1, m2, anchor, mom,
    probs, att, att_t, ds, delta, from_partner, pair, from_peers,
    in_sem,
    g_send, e_send, g_recv, p_send, p_recv, r_send, r_recv, a_send, a_recv, f_send, f_recv,
):
    heads = w.shape[0]
    width = g.shape[2]
    length = q.shape[0]
    slab = mom.shape[1]
    chips = workers // 2
    cw = width // CHUNKS
    scale = 1.0 / math.sqrt(DH)

    i = lax.axis_index("tensor")
    r = lax.axis_index("replica")
    chip = r // 2
    core = r % 2
    partner = chip * 2 + 1 - core
    has_left = i > 0
    has_right = i < tensors - 1

    def peer(step):
        return lax.rem(chip + step, chips) * 2 + core

    barrier = pltpu.get_barrier_semaphore()

    def other(step):
        return lax.rem(i + step, tensors)

    for step in range(1, tensors):
        pl.semaphore_signal(barrier, inc=1, device_id={"tensor": other(step)}, device_id_type=MESH)

    pl.semaphore_signal(barrier, inc=1, device_id={"replica": partner}, device_id_type=MESH)
    for step in range(1, chips):
        pl.semaphore_signal(barrier, inc=1, device_id={"replica": peer(step)}, device_id_type=MESH)

    loads = [
        pltpu.make_async_copy(s, d, in_sem.at[n])
        for n, (s, d) in enumerate(
            [
                (g_hbm, g.at[i]), (q_hbm, q), (k_hbm, k), (v_hbm, v), (w_hbm, w),
                (m1_hbm, m1), (m2_hbm, m2), (anchor_hbm, anchor), (mom_hbm, mom),
            ]
        )
    ]
    for load in loads:
        load.start()

    inner = jnp.logical_and(has_left, has_right)

    pl.semaphore_wait(barrier, tensors - 1 + chips)

    def cols(c):
        return pl.ds(pl.multiple_of(c * cw, cw), cw)

    def gather_copy(block, where, send, recv, target):
        piece = g.at[block, :, where]
        return pltpu.make_async_remote_copy(
            src_ref=piece, dst_ref=piece, send_sem=send, recv_sem=recv,
            device_id={"tensor": target}, device_id_type=MESH,
        )

    def right_copy(block, s, c):
        return gather_copy(block, cols(c), g_send.at[0, s], g_recv.at[block, c], i + 1)

    def left_copy(block, s, c):
        return gather_copy(block, cols(c), g_send.at[1, s], g_recv.at[block, c], i - 1)

    far_right = i < tensors - 2
    far_left = i > 1

    def own_first(c):
        if c < DIRECT:
            @pl.when(far_right)
            def _():
                gather_copy(i, cols(c), e_send.at[0], g_recv.at[i, c], tensors - 1).start()

            @pl.when(far_left)
            def _():
                gather_copy(i, cols(c), e_send.at[1], g_recv.at[i, c], 0).start()

        @pl.when(jnp.logical_and(has_right, jnp.logical_or(i == 0, c < AHEAD)))
        def _():
            right_copy(i, 0, c).start()

        @pl.when(jnp.logical_and(has_left, jnp.logical_or(i == tensors - 1, c < AHEAD)))
        def _():
            left_copy(i, 0, c).start()

    def own_later(n):
        c = n + AHEAD - SKEW * (i - 1)

        @pl.when(jnp.logical_and(inner, jnp.logical_and(c >= AHEAD, c < CHUNKS)))
        def _():
            right_copy(i, 0, c).start()

        e = n + AHEAD - SKEW * (tensors - 2 - i)

        @pl.when(jnp.logical_and(inner, jnp.logical_and(e >= AHEAD, e < CHUNKS)))
        def _():
            left_copy(i, 0, e).start()

    def relay(c, s):
        @pl.when(i - 1 - s >= 0)
        def _():
            block = i - 1 - s
            right_copy(block, s, c).wait_recv()
            if s + 1 <= tensors - 2:
                @pl.when(jnp.logical_or(far_right, c >= DIRECT))
                def _():
                    right_copy(block, s + 1, c).start()

        @pl.when(i + 1 + s < tensors)
        def _():
            block = i + 1 + s
            left_copy(block, s, c).wait_recv()
            if s + 1 <= tensors - 2:
                @pl.when(jnp.logical_or(far_left, c >= DIRECT))
                def _():
                    left_copy(block, s + 1, c).start()

    def arrive(c):
        for step in range(1, tensors):
            block = lax.rem(i + step, tensors)
            right_copy(block, 0, c).wait_recv()

    def drain_gather():
        start = pl.ds(0, DIRECT * cw)
        rest = pl.ds(DIRECT * cw, width - DIRECT * cw)
        every = pl.ds(0, width)
        if DIRECT > 0:
            @pl.when(far_right)
            def _():
                gather_copy(i, start, e_send.at[0], g_recv.at[i, 0], i).wait_send()

            @pl.when(far_left)
            def _():
                gather_copy(i, start, e_send.at[1], g_recv.at[i, 0], i).wait_send()

        for s in range(tensors - 1):
            for side, ok, far in ((0, has_right, far_right), (1, has_left, far_left)):
                block = i + s if side else i - s
                held = jnp.logical_and(block >= 0, block < tensors)
                ok = jnp.logical_and(ok, held)
                if s == 0:
                    far = ok

                @pl.when(jnp.logical_and(ok, far))
                def _():
                    gather_copy(block, every, g_send.at[side, s], g_recv.at[i, 0], i).wait_send()

                if s > 0:
                    @pl.when(jnp.logical_and(ok, jnp.logical_not(far)))
                    def _():
                        gather_copy(block, rest, g_send.at[side, s], g_recv.at[i, 0], i).wait_send()

    def head_cols(h):
        return pl.ds(pl.multiple_of(h * DH, DH), DH)

    def forward(h):
        hc = head_cols(h)
        s = dot(q[:, hc], k[:, hc], 1, 1) * scale
        e = jnp.exp(s - jnp.max(s, axis=-1, keepdims=True))
        p = (e / jnp.sum(e, axis=-1, keepdims=True)).astype(BF16)
        probs[h] = p
        a = dot(p, v[:, hc], 1, 0)
        att[:, hc] = a.astype(BF16)
        att_t[h] = a.T.astype(BF16)

    def adam(c):
        def body(h, carry):
            gb = g[:, :, cols(c)].reshape(length, cw)
            grad = dot(att_t[h], gb, 1, 0)
            first = beta_first * m1[h, :, cols(c)].astype(F32) + (1.0 - beta_first) * grad
            second = (
                beta_second * m2[h, :, cols(c)].astype(F32) + (1.0 - beta_second) * grad * grad
            )
            n1[h, :, cols(c)] = first.astype(BF16)
            n2[h, :, cols(c)] = second.astype(BF16)
            old = w[h, :, cols(c)].astype(F32)
            moved = (inner_rate / correct_first) * first / (
                jnp.sqrt(second * (1.0 / correct_second)) + epsilon
            )
            stepped = old * (1.0 - inner_rate * decay_rate) - moved
            an = anchor[h, :, :, cols(c)].astype(F32)
            d = an - stepped.reshape(workers, slab, cw)
            for x in range(workers):
                delta[c, x % 2, x // 2, h] = d[x].astype(BF16)
            return carry

        lax.fori_loop(0, heads, body, 0, unroll=UNROLL)

    def partner_copy(c):
        return pltpu.make_async_remote_copy(
            src_ref=delta.at[c, 1 - core], dst_ref=from_partner.at[c],
            send_sem=p_send, recv_sem=p_recv.at[c],
            device_id={"replica": partner}, device_id_type=MESH,
        )

    def peer_copy(c, step):
        return pltpu.make_async_remote_copy(
            src_ref=pair.at[c, lax.rem(chip + step, chips)], dst_ref=from_peers.at[c, step - 1],
            send_sem=r_send, recv_sem=r_recv.at[c],
            device_id={"replica": peer(step)}, device_id_type=MESH,
        )

    def pair_sum(c):
        partner_copy(c).wait_recv()
        for x in range(chips):
            pair[c, x] = (
                delta[c, core, x].astype(F32) + from_partner[c, x].astype(F32)
            ).astype(BF16)
        for step in range(1, chips):
            peer_copy(c, step).start()

    def spread(c, step):
        piece = na.at[:, chip, core, :, cols(c)]
        return pltpu.make_async_remote_copy(
            src_ref=piece, dst_ref=piece, send_sem=a_send, recv_sem=a_recv.at[c],
            device_id={"replica": peer(step)}, device_id_type=MESH,
        )

    def across(c, side):
        piece = na.at[:, :, side, :, cols(c)]
        return pltpu.make_async_remote_copy(
            src_ref=piece, dst_ref=piece, send_sem=f_send, recv_sem=f_recv.at[c],
            device_id={"replica": partner}, device_id_type=MESH,
        )

    def arrived(ref, sem):
        pltpu.make_async_copy(ref, ref, sem).wait()

    def outer(c):
        arrived(from_peers.at[c], r_recv.at[c])
        total = delta[c, core, chip].astype(F32) + from_partner[c, chip].astype(F32)
        for step in range(1, chips):
            total = total + from_peers[c, step - 1].astype(F32)
        average = total / workers
        moved = outer_beta * mom[:, :, cols(c)] + average
        nm[:, :, cols(c)] = moved
        part = anchor[:, r, :, cols(c)].astype(F32)
        na[:, chip, core, :, cols(c)] = (
            part - outer_rate * (average + outer_beta * moved)
        ).astype(BF16)
        for step in range(1, chips):
            spread(c, step).start()

    def pass_on(c):
        arrived(from_peers.at[c], a_recv.at[c])
        across(c, core).start()

    def finish(c):
        across(c, 1 - core).wait_recv()

    def backward(h):
        hc = head_cols(h)
        kh = k[:, hc]
        ga = dot(g[...].reshape(length, width), w[h], 1, 1).astype(BF16)
        row = jnp.sum(ga.astype(F32) * att[:, hc].astype(F32), axis=-1, keepdims=True)
        gp = dot(ga, v[:, hc], 1, 1)
        s = (probs[h].astype(F32) * (gp - row)).astype(BF16)
        ds[...] = s
        dq[:, hc] = (dot(s, kh, 1, 0) * scale).astype(BF16)
        dv[:, hc] = dot(ga, probs[h], 0, 0).T.astype(BF16)
        dk[:, hc] = (dot(q[:, hc], ds[...], 0, 0) * scale).T.astype(BF16)

    def within(n, count):
        return jnp.logical_and(n >= 0, n < count)

    loads[0].wait()
    for c in range(CHUNKS):
        own_first(c)
    for load in loads[1:4]:
        load.wait()
    for h in range(heads):
        forward(h)
    for load in loads[4:]:
        load.wait()

    far = jnp.maximum(i, tensors - 1 - i)
    lag = jnp.where(inner, SKEW * (far - 1) + MID, 0)
    early = jnp.where(inner, 0, DIRECT)
    summed = 1 + SUM_LAG
    spreads = summed + SPREAD_LAG

    def step(n, carry):
        for s in range(tensors - 1):
            c = n - SKEW * s

            @pl.when(jnp.logical_and(inner, within(c, CHUNKS)))
            def _():
                relay(c, s)

        own_later(n)

        m = n - lag

        if DIRECT > 0:
            @pl.when(jnp.logical_and(jnp.logical_not(inner), m == DIRECT))
            def _():
                pair_sum(DIRECT - 1)
                for c in range(DIRECT):
                    outer(c)
                for c in range(DIRECT):
                    pass_on(c)

        @pl.when(within(m, CHUNKS))
        def _():
            @pl.when(jnp.logical_not(inner))
            def _():
                arrive(m)

            adam(m)
            partner_copy(m).start()

        @pl.when(within(m - CHUNKS, heads))
        def _():
            backward(m - CHUNKS)

        @pl.when(jnp.logical_and(within(m - 1, CHUNKS), m != early))
        def _():
            pair_sum(m - 1)

        @pl.when(jnp.logical_and(m - summed >= early, m - summed < CHUNKS))
        def _():
            outer(m - summed)

        @pl.when(jnp.logical_and(m - spreads >= early, m - spreads < CHUNKS))
        def _():
            pass_on(m - spreads)

        return carry

    longest = SKEW * max(tensors - 3, 0) + MID
    lax.fori_loop(0, longest + CHUNKS + max(spreads, heads), step, 0)
    for c in range(CHUNKS):
        finish(c)
    drain_gather()
    arrived(from_partner, p_send)
    arrived(from_peers, r_send)
    arrived(from_peers, a_send)
    arrived(from_partner, f_send)


def store(*refs):
    n = (len(refs) - 1) // 2
    copies = [pltpu.make_async_copy(refs[j], refs[n + j], refs[-1].at[j]) for j in range(n)]
    for copy in copies:
        copy.start()
    for copy in copies:
        copy.wait()


def local(tensors, workers, queries, key_rows, value_rows, out_grads, inner_weights, adam_first,
          adam_second, anchor, momentum):
    length, inner = queries.shape[1:]
    rows, width = out_grads.shape[1:]
    heads = inner_weights.shape[1]
    slab = momentum.shape[1]
    chips = workers // 2
    cw = width // CHUNKS
    qs = (length, inner)
    ws = (heads, DH, width)
    an = (heads, workers, slab, width)
    ms = (heads, slab, width)
    S = jax.ShapeDtypeStruct
    hbm = pl.BlockSpec(memory_space=pltpu.HBM)
    V = pltpu.VMEM
    D = pltpu.SemaphoreType.DMA
    nas = (heads, chips, 2, slab, width)
    results = [(qs, BF16)] * 3 + [(ws, BF16)] * 2 + [(nas, BF16), (ms, F32)]
    held = sum(math.prod(shape) * jnp.dtype(dtype).itemsize for shape, dtype in results)
    room = VMEM_BYTES - held - SPARE
    outs = pl.pallas_call(
        functools.partial(kernel, tensors, workers),
        out_shape=[V(shape, dtype) for shape, dtype in results],
        in_specs=[hbm] * 9,
        out_specs=[pl.BlockSpec(memory_space=V)] * 7,
        scratch_shapes=[
            V(qs, BF16), V(qs, BF16), V(qs, BF16), V((tensors, rows, width), BF16),
            V(ws, BF16), V(ws, BF16), V(ws, BF16), V(an, BF16), V(ms, F32),
            V((heads, length, length), BF16), V(qs, BF16), V((heads, DH, length), BF16),
            V((length, length), BF16),
            V((CHUNKS, 2, chips, heads, slab, cw), BF16),
            V((CHUNKS, chips, heads, slab, cw), BF16),
            V((CHUNKS, chips, heads, slab, cw), BF16),
            V((CHUNKS, chips - 1, heads, slab, cw), BF16),
            D((9,)),
            D((2, tensors - 1)), D((2,)), D((tensors, CHUNKS)),
            D, D((CHUNKS,)), D, D((CHUNKS,)), D, D((CHUNKS,)), D, D((CHUNKS,)),
        ],
        compiler_params=pltpu.CompilerParams(collective_id=0, has_side_effects=True, vmem_limit_bytes=room),
        name="sync",
    )(
        queries[0], key_rows[0], value_rows[0], out_grads[0], inner_weights[0], adam_first[0],
        adam_second[0], anchor.reshape(an), momentum,
    )
    dq, dk, dv, n1, n2, na, nm = pl.pallas_call(
        store,
        out_shape=[S(shape, dtype) for shape, dtype in results],
        in_specs=[pl.BlockSpec(memory_space=V)] * 7,
        out_specs=[hbm] * 7,
        scratch_shapes=[D((7,))],
        compiler_params=pltpu.CompilerParams(vmem_limit_bytes=2**20),
        name="store",
    )(*outs)
    return dq[None], dk[None], dv[None], n1[None], n2[None], na.reshape(anchor.shape), nm


def solution(mesh):
    workers = P("replica", "tensor", None, None)
    heads = P("replica", None, "tensor")
    specs = (
        heads, heads, heads, P("replica", "tensor", None), workers, workers, workers,
        P("tensor", None, None), P("tensor", "replica", None),
    )
    outs = (
        heads, heads, heads, workers, workers, P("tensor", None, None), P("tensor", "replica", None)
    )
    body = functools.partial(local, mesh.shape["tensor"], mesh.shape["replica"])
    return jax.shard_map(body, mesh=mesh, in_specs=specs, out_specs=outs, check_vma=False)
```

```python
import functools
import math

import jax
import jax.numpy as jnp
from jax import lax
from jax.experimental import pallas as pl
from jax.experimental.pallas import tpu as pltpu
from jax.sharding import PartitionSpec as P

DH = 128
CHUNKS = 8
DIRECT = 2
AHEAD = 3
AHEAD_END = 6
AHEAD1 = 4
AHEAD_END1 = 5
SKEW = 2
SUM_LAG = 3
SPREAD_LAG = 6
UNROLL = 5
MID = 0
RIGHT = 0
TURN = 2
EARLY = 2
NEAR_AT = 1
FAR_AT = 3
VMEM_BYTES = 67043328
SPARE = 2**17
MESH = pl.DeviceIdType.MESH

beta_first = 0.9
beta_second = 0.95
correct_first = 0.9999734386011124
correct_second = 0.994079470779666
inner_rate = 0.01
decay_rate = 0.1
epsilon = 1e-08
outer_rate = 0.7
outer_beta = 0.9

F32 = jnp.float32
BF16 = jnp.bfloat16


def dot(a, b, ca, cb):
    return lax.dot_general(a, b, (((ca,), (cb,)), ((), ())), preferred_element_type=F32)


def kernel(
    tensors,
    workers,
    q_hbm, k_hbm, v_hbm, g_hbm, w_hbm, m1_hbm, m2_hbm, anchor_hbm, mom_hbm,
    dq, dk, dv, n1, n2, na, nm,
    q, k, v, g, w, m1, m2, anchor, mom,
    probs, att, att_t, ds, gs, gacc, delta, from_partner, pair, from_peers,
    in_sem,
    near, far_end, side, g_send, e_send, g_recv, p_send, p_recv, r_send, r_recv, a_send, a_recv, f_send, f_recv,
):
    heads = w.shape[0]
    width = g.shape[2]
    length = q.shape[0]
    slab = mom.shape[1]
    chips = workers // 2
    cw = width // CHUNKS
    scale = 1.0 / math.sqrt(DH)

    i = lax.axis_index("tensor")
    r = lax.axis_index("replica")
    chip = r // 2
    core = r % 2
    partner = chip * 2 + 1 - core
    has_left = i > 0
    has_right = i < tensors - 1

    def peer(step):
        return lax.rem(chip + step, chips) * 2 + core

    barrier = pltpu.get_barrier_semaphore()

    for step in range(1, tensors):
        @pl.when(i + step < tensors)
        def _():
            pl.semaphore_signal(barrier, inc=1, device_id={"tensor": i + step}, device_id_type=MESH)

    @pl.when(core == 0)
    def _():
        pl.semaphore_signal(barrier, inc=1, device_id={"replica": partner}, device_id_type=MESH)

    for step in range(1, chips):
        @pl.when(chip + step < chips)
        def _():
            pl.semaphore_signal(barrier, inc=1, device_id={"replica": peer(step)}, device_id_type=MESH)

    loads = [
        pltpu.make_async_copy(s, d, in_sem.at[n])
        for n, (s, d) in enumerate(
            [
                (g_hbm, g.at[i]), (q_hbm, q), (k_hbm, k), (v_hbm, v), (w_hbm, w),
                (m1_hbm, m1), (m2_hbm, m2), (anchor_hbm, anchor), (mom_hbm, mom),
            ]
        )
    ]
    for load in loads:
        load.start()

    inner = jnp.logical_and(has_left, has_right)

    @pl.when(i + chip + core > 0)
    def _():
        pl.semaphore_wait(barrier, i + chip + core)

    @pl.when(has_left)
    def _():
        pl.semaphore_signal(near, inc=1, device_id={"tensor": i - 1}, device_id_type=MESH)

    @pl.when(core == 1)
    def _():
        pl.semaphore_signal(side, inc=1, device_id={"replica": partner}, device_id_type=MESH)

    for step in range(1, chips):
        @pl.when(chip + step >= chips)
        def _():
            pl.semaphore_signal(side, inc=1, device_id={"replica": peer(step)}, device_id_type=MESH)

    for step in range(2, tensors):
        @pl.when(jnp.logical_and(i == tensors - 1, i - step >= 0))
        def _():
            pl.semaphore_signal(far_end, inc=1, device_id={"tensor": i - step}, device_id_type=MESH)

    def cols(c):
        return pl.ds(pl.multiple_of(c * cw, cw), cw)

    def gather_copy(block, where, send, recv, target):
        piece = g.at[block, :, where]
        return pltpu.make_async_remote_copy(
            src_ref=piece, dst_ref=piece, send_sem=send, recv_sem=recv,
            device_id={"tensor": target}, device_id_type=MESH,
        )

    def right_copy(block, s, c):
        return gather_copy(block, cols(c), g_send.at[0, s], g_recv.at[block, c], i + 1)

    def left_copy(block, s, c):
        return gather_copy(block, cols(c), g_send.at[1, s], g_recv.at[block, c], i - 1)

    far_right = i < tensors - 2
    far_left = i > 1

    def turned(c):
        return lax.rem(c + TURN, CHUNKS)

    def own_right(n):
        right_copy(i, 0, jnp.where(far_right, turned(n), n)).start()

    def own_left(n):
        left_copy(i, 0, jnp.where(far_left, turned(n), n)).start()

    ahead = jnp.where(core == 0, AHEAD, AHEAD1)
    ahead_end = jnp.where(core == 0, AHEAD_END, AHEAD_END1)
    ahead_right = jnp.where(i == 0, CHUNKS, jnp.where(far_right, ahead, ahead_end))
    ahead_left = jnp.where(i == tensors - 1, CHUNKS, jnp.where(far_left, ahead, ahead_end))

    def first_left():
        for n in range(CHUNKS):
            @pl.when(jnp.logical_and(i == 1, n < ahead_left))
            def _():
                own_left(n)

            if n < DIRECT:
                @pl.when(far_left)
                def _():
                    gather_copy(i, cols(n), e_send.at[1], g_recv.at[i, n], 0).start()

        for n in range(CHUNKS):
            @pl.when(jnp.logical_and(far_left, n < ahead_left))
            def _():
                own_left(n)

    def first_near():
        @pl.when(has_right)
        def _():
            pl.semaphore_wait(near, 1)

        for n in range(CHUNKS):
            @pl.when(jnp.logical_and(has_right, n < ahead_right))
            def _():
                own_right(n)

    def first_far():
        @pl.when(far_right)
        def _():
            pl.semaphore_wait(far_end, 1)

        for n in range(DIRECT):
            @pl.when(far_right)
            def _():
                gather_copy(i, cols(n), e_send.at[0], g_recv.at[i, n], tensors - 1).start()

    def later_right(n):
        c = n + ahead_right - SKEW * (i - 1)

        @pl.when(jnp.logical_and(inner, jnp.logical_and(c >= ahead_right, c < CHUNKS)))
        def _():
            own_right(c)

    def later_left(n):
        c = n + ahead_left - SKEW * (tensors - 2 - i)

        @pl.when(jnp.logical_and(inner, jnp.logical_and(c >= ahead_left, c < CHUNKS)))
        def _():
            own_left(c)

    def relay_right(c, s):
        block = i - 1 - s
        right_copy(block, s, c).wait_recv()
        if s + 1 <= tensors - 2:
            @pl.when(jnp.logical_or(far_right, c >= DIRECT))
            def _():
                right_copy(block, s + 1, c).start()

    def relay_left(c, s):
        block = i + 1 + s
        left_copy(block, s, c).wait_recv()
        if s + 1 <= tensors - 2:
            @pl.when(jnp.logical_or(far_left, c >= DIRECT))
            def _():
                left_copy(block, s + 1, c).start()

    def arrive(c):
        for step in range(1, tensors):
            block = lax.rem(i + step, tensors)
            right_copy(block, 0, c).wait_recv()

    def drain_gather():
        start = pl.ds(0, DIRECT * cw)
        rest = pl.ds(DIRECT * cw, width - DIRECT * cw)
        every = pl.ds(0, width)
        if DIRECT > 0:
            @pl.when(far_right)
            def _():
                gather_copy(i, start, e_send.at[0], g_recv.at[i, 0], i).wait_send()

            @pl.when(far_left)
            def _():
                gather_copy(i, start, e_send.at[1], g_recv.at[i, 0], i).wait_send()

        for s in range(tensors - 1):
            for side, ok, far in ((0, has_right, far_right), (1, has_left, far_left)):
                block = i + s if side else i - s
                held = jnp.logical_and(block >= 0, block < tensors)
                ok = jnp.logical_and(ok, held)
                if s == 0:
                    far = ok

                @pl.when(jnp.logical_and(ok, far))
                def _():
                    gather_copy(block, every, g_send.at[side, s], g_recv.at[i, 0], i).wait_send()

                if s > 0:
                    @pl.when(jnp.logical_and(ok, jnp.logical_not(far)))
                    def _():
                        gather_copy(block, rest, g_send.at[side, s], g_recv.at[i, 0], i).wait_send()

    def head_cols(h):
        return pl.ds(pl.multiple_of(h * DH, DH), DH)

    def forward(h):
        hc = head_cols(h)
        s = dot(q[:, hc], k[:, hc], 1, 1) * scale
        e = jnp.exp(s - jnp.max(s, axis=-1, keepdims=True))
        p = (e / jnp.sum(e, axis=-1, keepdims=True)).astype(BF16)
        probs[h] = p
        a = dot(p, v[:, hc], 1, 0)
        att[:, hc] = a.astype(BF16)
        att_t[h] = a.T.astype(BF16)

    def adam(c):
        def body(h, carry):
            gb = g[:, :, cols(c)].reshape(length, cw)
            grad = dot(att_t[h], gb, 1, 0)
            first = beta_first * m1[h, :, cols(c)].astype(F32) + (1.0 - beta_first) * grad
            second = (
                beta_second * m2[h, :, cols(c)].astype(F32) + (1.0 - beta_second) * grad * grad
            )
            n1[h, :, cols(c)] = first.astype(BF16)
            n2[h, :, cols(c)] = second.astype(BF16)
            old = w[h, :, cols(c)].astype(F32)
            power = second * (1.0 / correct_second)
            moved = (inner_rate / correct_first) * first / (power * lax.rsqrt(power) + epsilon)
            stepped = old * (1.0 - inner_rate * decay_rate) - moved
            an = anchor[h, :, :, cols(c)].astype(F32)
            d = an - stepped.reshape(workers, slab, cw)
            for x in range(workers):
                delta[c, x % 2, x // 2, h] = d[x].astype(BF16)
            return carry

        lax.fori_loop(0, heads, body, 0, unroll=UNROLL)

    def partner_copy(c):
        return pltpu.make_async_remote_copy(
            src_ref=delta.at[c, 1 - core], dst_ref=from_partner.at[c],
            send_sem=p_send, recv_sem=p_recv.at[c],
            device_id={"replica": partner}, device_id_type=MESH,
        )

    def peer_copy(c, step):
        return pltpu.make_async_remote_copy(
            src_ref=pair.at[c, lax.rem(chip + step, chips)], dst_ref=from_peers.at[c, step - 1],
            send_sem=r_send, recv_sem=r_recv.at[c],
            device_id={"replica": peer(step)}, device_id_type=MESH,
        )

    def pair_sum(c):
        partner_copy(c).wait_recv()
        for x in range(chips):
            pair[c, x] = (
                delta[c, core, x].astype(F32) + from_partner[c, x].astype(F32)
            ).astype(BF16)
        for step in range(1, chips):
            peer_copy(c, step).start()

    def spread(c, step):
        piece = na.at[:, chip, core, :, cols(c)]
        return pltpu.make_async_remote_copy(
            src_ref=piece, dst_ref=piece, send_sem=a_send, recv_sem=a_recv.at[c],
            device_id={"replica": peer(step)}, device_id_type=MESH,
        )

    def across(c, side):
        piece = na.at[:, :, side, :, cols(c)]
        return pltpu.make_async_remote_copy(
            src_ref=piece, dst_ref=piece, send_sem=f_send, recv_sem=f_recv.at[c],
            device_id={"replica": partner}, device_id_type=MESH,
        )

    def arrived(ref, sem):
        pltpu.make_async_copy(ref, ref, sem).wait()

    def outer(c):
        arrived(from_peers.at[c], r_recv.at[c])
        total = delta[c, core, chip].astype(F32) + from_partner[c, chip].astype(F32)
        for step in range(1, chips):
            total = total + from_peers[c, step - 1].astype(F32)
        average = total / workers
        moved = outer_beta * mom[:, :, cols(c)] + average
        nm[:, :, cols(c)] = moved
        part = anchor[:, r, :, cols(c)].astype(F32)
        na[:, chip, core, :, cols(c)] = (
            part - outer_rate * (average + outer_beta * moved)
        ).astype(BF16)
        for step in range(1, chips):
            spread(c, step).start()

    def pass_on(c):
        arrived(from_peers.at[c], a_recv.at[c])
        across(c, core).start()

    def finish(c):
        across(c, 1 - core).wait_recv()

    def weigh(c):
        part = pl.ds(pl.multiple_of(c * cw, cw), 2 * cw)
        return dot(
            g[:, :, part].reshape(length, 2 * cw), w[:, :, part].reshape(heads * DH, 2 * cw), 1, 1
        )

    def backward(h):
        hc = head_cols(h)
        kh = k[:, hc]
        ga = gs[:, hc]
        row = jnp.sum(ga.astype(F32) * att[:, hc].astype(F32), axis=-1, keepdims=True)
        gp = dot(ga, v[:, hc], 1, 1)
        s = (probs[h].astype(F32) * (gp - row)).astype(BF16)
        ds[...] = s
        dq[:, hc] = (dot(s, kh, 1, 0) * scale).astype(BF16)
        dv[:, hc] = dot(ga, probs[h], 0, 0).T.astype(BF16)
        dk[:, hc] = (dot(q[:, hc], ds[...], 0, 0) * scale).T.astype(BF16)

    def within(n, count):
        return jnp.logical_and(n >= 0, n < count)

    loads[0].wait()
    first_left()
    for load in loads[1:4]:
        load.wait()
    for h in range(heads):
        if h == min(NEAR_AT, heads - 1):
            first_near()
        if h == min(FAR_AT, heads - 1):
            first_far()
        forward(h)
    for load in loads[4:]:
        load.wait()

    @pl.when(chips - chip - core > 0)
    def _():
        pl.semaphore_wait(side, chips - chip - core)


    behind = jnp.maximum(SKEW * (i - 1) + RIGHT, SKEW * (tensors - 2 - i))
    lag = jnp.where(inner, behind + MID, 0)
    early = jnp.where(inner, 0, EARLY)
    summed = 1 + SUM_LAG
    spreads = summed + SPREAD_LAG

    def order(c):
        return jnp.where(inner, turned(c), c)

    def step(n, carry):
        for s in range(tensors - 1):
            c = n - SKEW * s

            @pl.when(jnp.logical_and(inner, jnp.logical_and(i + 1 + s < tensors, within(c, CHUNKS))))
            def _():
                relay_left(turned(c), s)

        later_left(n)
        for s in range(tensors - 1):
            c = n - RIGHT - SKEW * s

            @pl.when(jnp.logical_and(inner, jnp.logical_and(i - 1 - s >= 0, within(c, CHUNKS))))
            def _():
                relay_right(turned(c), s)

        later_right(n - RIGHT)

        m = n - lag

        @pl.when(jnp.logical_and(jnp.logical_not(inner), m == DIRECT))
        def _():
            if DIRECT > 0:
                pair_sum(DIRECT - 1)
            for c in range(EARLY):
                outer(c)

        @pl.when(within(m, CHUNKS))
        def _():
            @pl.when(jnp.logical_not(inner))
            def _():
                arrive(m)

            adam(order(m))
            partner_copy(order(m)).start()

        @pl.when(m == 2)
        def _():
            gacc[...] = weigh(order(0))

        @pl.when(jnp.logical_and(lax.rem(m + CHUNKS, 2) == 0, jnp.logical_and(m > 2, m < CHUNKS - 2)))
        def _():
            gacc[...] += weigh(order(m - 2))

        @pl.when(m == CHUNKS)
        def _():
            gs[...] = (gacc[...] + weigh(order(CHUNKS - 4)) + weigh(order(CHUNKS - 2))).astype(BF16)

        @pl.when(within(m - CHUNKS - 1, heads))
        def _():
            backward(m - CHUNKS - 1)

        @pl.when(jnp.logical_and(within(m - 1, CHUNKS), jnp.logical_or(inner, m != DIRECT)))
        def _():
            pair_sum(order(m - 1))

        @pl.when(jnp.logical_and(m - summed >= early, m - summed < CHUNKS))
        def _():
            outer(order(m - summed))

        @pl.when(within(m - spreads, CHUNKS))
        def _():
            pass_on(order(m - spreads))

        return carry

    longest = SKEW * max(tensors - 3, 0) + RIGHT + MID
    lax.fori_loop(0, longest + CHUNKS + max(spreads, heads + 1), step, 0)
    for c in range(CHUNKS):
        finish(c)
    drain_gather()
    arrived(from_partner, p_send)
    arrived(from_peers, r_send)
    arrived(from_peers, a_send)
    arrived(from_partner, f_send)


def store(*refs):
    n = (len(refs) - 1) // 2
    copies = [pltpu.make_async_copy(refs[j], refs[n + j], refs[-1].at[j]) for j in range(n)]
    for copy in copies:
        copy.start()
    for copy in copies:
        copy.wait()


def local(tensors, workers, queries, key_rows, value_rows, out_grads, inner_weights, adam_first,
          adam_second, anchor, momentum):
    length, inner = queries.shape[1:]
    rows, width = out_grads.shape[1:]
    heads = inner_weights.shape[1]
    slab = momentum.shape[1]
    chips = workers // 2
    cw = width // CHUNKS
    qs = (length, inner)
    ws = (heads, DH, width)
    an = (heads, workers, slab, width)
    ms = (heads, slab, width)
    S = jax.ShapeDtypeStruct
    hbm = pl.BlockSpec(memory_space=pltpu.HBM)
    V = pltpu.VMEM
    D = pltpu.SemaphoreType.DMA
    nas = (heads, chips, 2, slab, width)
    results = [(qs, BF16)] * 3 + [(ws, BF16)] * 2 + [(nas, BF16), (ms, F32)]
    held = sum(math.prod(shape) * jnp.dtype(dtype).itemsize for shape, dtype in results)
    room = VMEM_BYTES - held - SPARE
    outs = pl.pallas_call(
        functools.partial(kernel, tensors, workers),
        out_shape=[V(shape, dtype) for shape, dtype in results],
        in_specs=[hbm] * 9,
        out_specs=[pl.BlockSpec(memory_space=V)] * 7,
        scratch_shapes=[
            V(qs, BF16), V(qs, BF16), V(qs, BF16), V((tensors, rows, width), BF16),
            V(ws, BF16), V(ws, BF16), V(ws, BF16), V(an, BF16), V(ms, F32),
            V((heads, length, length), BF16), V(qs, BF16), V((heads, DH, length), BF16),
            V((length, length), BF16), V((length, heads * DH), BF16), V((length, heads * DH), F32),
            V((CHUNKS, 2, chips, heads, slab, cw), BF16),
            V((CHUNKS, chips, heads, slab, cw), BF16),
            V((CHUNKS, chips, heads, slab, cw), BF16),
            V((CHUNKS, chips - 1, heads, slab, cw), BF16),
            D((9,)),
            pltpu.SemaphoreType.REGULAR, pltpu.SemaphoreType.REGULAR, pltpu.SemaphoreType.REGULAR,
            D((2, tensors - 1)), D((2,)), D((tensors, CHUNKS)),
            D, D((CHUNKS,)), D, D((CHUNKS,)), D, D((CHUNKS,)), D, D((CHUNKS,)),
        ],
        compiler_params=pltpu.CompilerParams(collective_id=0, has_side_effects=True, vmem_limit_bytes=room),
        name="sync",
    )(
        queries[0], key_rows[0], value_rows[0], out_grads[0], inner_weights[0], adam_first[0],
        adam_second[0], anchor.reshape(an), momentum,
    )
    dq, dk, dv, n1, n2, na, nm = pl.pallas_call(
        store,
        out_shape=[S(shape, dtype) for shape, dtype in results],
        in_specs=[pl.BlockSpec(memory_space=V)] * 7,
        out_specs=[hbm] * 7,
        scratch_shapes=[D((7,))],
        compiler_params=pltpu.CompilerParams(vmem_limit_bytes=2**20),
        name="store",
    )(*outs)
    return dq[None], dk[None], dv[None], n1[None], n2[None], na.reshape(anchor.shape), nm


def solution(mesh):
    workers = P("replica", "tensor", None, None)
    heads = P("replica", None, "tensor")
    specs = (
        heads, heads, heads, P("replica", "tensor", None), workers, workers, workers,
        P("tensor", None, None), P("tensor", "replica", None),
    )
    outs = (
        heads, heads, heads, workers, workers, P("tensor", None, None), P("tensor", "replica", None)
    )
    body = functools.partial(local, mesh.shape["tensor"], mesh.shape["replica"])
    return jax.shard_map(body, mesh=mesh, in_specs=specs, out_specs=outs, check_vma=False)
```

```python
import functools
import math

import jax
import jax.numpy as jnp
from jax import lax
from jax.experimental import pallas as pl
from jax.experimental.pallas import tpu as pltpu
from jax.sharding import PartitionSpec as P

DH = 128
CHUNKS = 8
DIRECT = 2
AHEAD = 3
AHEAD_END = 7
AHEAD1 = 4
AHEAD_END1 = 5
SKEW = 2
SUM_LAG = 3
SPREAD_LAG = 6
UNROLL = 5
MID = 0
RIGHT = 0
TURN = 2
SKEW_RIGHT = 2
RIGHT_FIRST = True
EARLY = 2
NEAR_AT = 1
FAR_AT = 3
VMEM_BYTES = 67043328
SPARE = 2**17
MESH = pl.DeviceIdType.MESH

beta_first = 0.9
beta_second = 0.95
correct_first = 0.9999734386011124
correct_second = 0.994079470779666
inner_rate = 0.01
decay_rate = 0.1
epsilon = 1e-08
outer_rate = 0.7
outer_beta = 0.9

F32 = jnp.float32
BF16 = jnp.bfloat16


def dot(a, b, ca, cb):
    return lax.dot_general(a, b, (((ca,), (cb,)), ((), ())), preferred_element_type=F32)


def kernel(
    tensors,
    workers,
    q_hbm, k_hbm, v_hbm, g_hbm, w_hbm, m1_hbm, m2_hbm, anchor_hbm, mom_hbm,
    dq, dk, dv, n1, n2, na, nm,
    q, k, v, g, w, m1, m2, anchor, mom,
    probs, att, att_t, ds, gs, gacc, delta, from_partner, pair, from_peers,
    in_sem,
    near, far_end, side, g_send, e_send, g_recv, p_send, p_recv, r_send, r_recv, a_send, a_recv, f_send, f_recv,
):
    heads = w.shape[0]
    width = g.shape[2]
    length = q.shape[0]
    slab = mom.shape[1]
    chips = workers // 2
    cw = width // CHUNKS
    scale = 1.0 / math.sqrt(DH)

    i = lax.axis_index("tensor")
    r = lax.axis_index("replica")
    chip = r // 2
    core = r % 2
    partner = chip * 2 + 1 - core
    has_left = i > 0
    has_right = i < tensors - 1

    def peer(step):
        return lax.rem(chip + step, chips) * 2 + core

    barrier = pltpu.get_barrier_semaphore()

    for step in range(1, tensors):
        @pl.when(i + step < tensors)
        def _():
            pl.semaphore_signal(barrier, inc=1, device_id={"tensor": i + step}, device_id_type=MESH)

    @pl.when(core == 0)
    def _():
        pl.semaphore_signal(barrier, inc=1, device_id={"replica": partner}, device_id_type=MESH)

    for step in range(1, chips):
        @pl.when(chip + step < chips)
        def _():
            pl.semaphore_signal(barrier, inc=1, device_id={"replica": peer(step)}, device_id_type=MESH)

    loads = [
        pltpu.make_async_copy(s, d, in_sem.at[n])
        for n, (s, d) in enumerate(
            [
                (g_hbm, g.at[i]), (q_hbm, q), (k_hbm, k), (v_hbm, v), (w_hbm, w),
                (m1_hbm, m1), (m2_hbm, m2), (anchor_hbm, anchor), (mom_hbm, mom),
            ]
        )
    ]
    for load in loads:
        load.start()

    inner = jnp.logical_and(has_left, has_right)

    @pl.when(i + chip + core > 0)
    def _():
        pl.semaphore_wait(barrier, i + chip + core)

    @pl.when(has_left)
    def _():
        pl.semaphore_signal(near, inc=1, device_id={"tensor": i - 1}, device_id_type=MESH)

    @pl.when(core == 1)
    def _():
        pl.semaphore_signal(side, inc=1, device_id={"replica": partner}, device_id_type=MESH)

    for step in range(1, chips):
        @pl.when(chip + step >= chips)
        def _():
            pl.semaphore_signal(side, inc=1, device_id={"replica": peer(step)}, device_id_type=MESH)

    for step in range(2, tensors):
        @pl.when(jnp.logical_and(i == tensors - 1, i - step >= 0))
        def _():
            pl.semaphore_signal(far_end, inc=1, device_id={"tensor": i - step}, device_id_type=MESH)

    def cols(c):
        return pl.ds(pl.multiple_of(c * cw, cw), cw)

    def gather_copy(block, where, send, recv, target):
        piece = g.at[block, :, where]
        return pltpu.make_async_remote_copy(
            src_ref=piece, dst_ref=piece, send_sem=send, recv_sem=recv,
            device_id={"tensor": target}, device_id_type=MESH,
        )

    def right_copy(block, s, c):
        return gather_copy(block, cols(c), g_send.at[0, s], g_recv.at[block, c], i + 1)

    def left_copy(block, s, c):
        return gather_copy(block, cols(c), g_send.at[1, s], g_recv.at[block - 1, c], i - 1)

    far_right = i < tensors - 2
    far_left = i > 1

    def turned(c):
        return lax.rem(c + TURN, CHUNKS)

    def own_right(n):
        right_copy(i, 0, jnp.where(far_right, turned(n), n)).start()

    def own_left(n):
        left_copy(i, 0, jnp.where(far_left, turned(n), n)).start()

    ahead = jnp.where(core == 0, AHEAD, AHEAD1)
    ahead_end = jnp.where(core == 0, AHEAD_END, AHEAD_END1)
    ahead_right = jnp.where(i == 0, CHUNKS, jnp.where(far_right, ahead, ahead_end))
    ahead_left = jnp.where(i == tensors - 1, CHUNKS, jnp.where(far_left, ahead, ahead_end))

    def first_left():
        for n in range(CHUNKS):
            @pl.when(jnp.logical_and(i == 1, n < ahead_left))
            def _():
                own_left(n)

            if n < DIRECT:
                @pl.when(far_left)
                def _():
                    gather_copy(i, cols(n), e_send.at[1], g_recv.at[i - 1, n], 0).start()

        for n in range(CHUNKS):
            @pl.when(jnp.logical_and(far_left, n < ahead_left))
            def _():
                own_left(n)

    def first_near():
        @pl.when(has_right)
        def _():
            pl.semaphore_wait(near, 1)

        for n in range(CHUNKS):
            @pl.when(jnp.logical_and(has_right, n < ahead_right))
            def _():
                own_right(n)

    def first_far():
        @pl.when(far_right)
        def _():
            pl.semaphore_wait(far_end, 1)

        for n in range(DIRECT):
            @pl.when(far_right)
            def _():
                gather_copy(i, cols(n), e_send.at[0], g_recv.at[i, n], tensors - 1).start()

    def later_right(n):
        c = n + ahead_right - SKEW_RIGHT * (i - 1)

        @pl.when(jnp.logical_and(inner, jnp.logical_and(c >= ahead_right, c < CHUNKS)))
        def _():
            own_right(c)

    def later_left(n):
        c = n + ahead_left - SKEW * (tensors - 2 - i)

        @pl.when(jnp.logical_and(inner, jnp.logical_and(c >= ahead_left, c < CHUNKS)))
        def _():
            own_left(c)

    def relay_right(c, s):
        block = i - 1 - s
        right_copy(block, s, c).wait_recv()
        if s + 1 <= tensors - 2:
            @pl.when(jnp.logical_or(far_right, c >= DIRECT))
            def _():
                right_copy(block, s + 1, c).start()

    def relay_left(c, s):
        block = i + 1 + s
        left_copy(block, s, c).wait_recv()
        if s + 1 <= tensors - 2:
            @pl.when(jnp.logical_or(far_left, c >= DIRECT))
            def _():
                left_copy(block, s + 1, c).start()

    def arrive(c):
        for step in range(1, tensors):
            block = lax.rem(i + step, tensors)
            arrived(g.at[block, :, cols(c)], g_recv.at[block - jnp.where(block > i, 1, 0), c])

    def drain_gather():
        start = pl.ds(0, DIRECT * cw)
        rest = pl.ds(DIRECT * cw, width - DIRECT * cw)
        every = pl.ds(0, width)
        if DIRECT > 0:
            @pl.when(far_right)
            def _():
                gather_copy(i, start, e_send.at[0], g_recv.at[0, 0], i).wait_send()

            @pl.when(far_left)
            def _():
                gather_copy(i, start, e_send.at[1], g_recv.at[0, 0], i).wait_send()

        for s in range(tensors - 1):
            for side, ok, far in ((0, has_right, far_right), (1, has_left, far_left)):
                block = i + s if side else i - s
                held = jnp.logical_and(block >= 0, block < tensors)
                ok = jnp.logical_and(ok, held)
                if s == 0:
                    far = ok

                @pl.when(jnp.logical_and(ok, far))
                def _():
                    gather_copy(block, every, g_send.at[side, s], g_recv.at[0, 0], i).wait_send()

                if s > 0:
                    @pl.when(jnp.logical_and(ok, jnp.logical_not(far)))
                    def _():
                        gather_copy(block, rest, g_send.at[side, s], g_recv.at[0, 0], i).wait_send()

    def head_cols(h):
        return pl.ds(pl.multiple_of(h * DH, DH), DH)

    def forward(h):
        hc = head_cols(h)
        s = dot(q[:, hc], k[:, hc], 1, 1) * scale
        e = jnp.exp(s - jnp.max(s, axis=-1, keepdims=True))
        p = (e / jnp.sum(e, axis=-1, keepdims=True)).astype(BF16)
        probs[h] = p
        a = dot(p, v[:, hc], 1, 0)
        att[:, hc] = a.astype(BF16)
        att_t[h] = a.T.astype(BF16)

    def adam(c):
        def body(h, carry):
            gb = g[:, :, cols(c)].reshape(length, cw)
            grad = dot(att_t[h], gb, 1, 0)
            first = beta_first * m1[h, :, cols(c)].astype(F32) + (1.0 - beta_first) * grad
            second = (
                beta_second * m2[h, :, cols(c)].astype(F32) + (1.0 - beta_second) * grad * grad
            )
            n1[h, :, cols(c)] = first.astype(BF16)
            n2[h, :, cols(c)] = second.astype(BF16)
            old = w[h, :, cols(c)].astype(F32)
            power = second * (1.0 / correct_second)
            moved = (inner_rate / correct_first) * first / (power * lax.rsqrt(power) + epsilon)
            stepped = old * (1.0 - inner_rate * decay_rate) - moved
            an = anchor[h, :, :, cols(c)].astype(F32)
            d = an - stepped.reshape(workers, slab, cw)
            for x in range(workers):
                delta[c, x % 2, x // 2, h] = d[x].astype(BF16)
            return carry

        lax.fori_loop(0, heads, body, 0, unroll=UNROLL)

    def partner_copy(c):
        return pltpu.make_async_remote_copy(
            src_ref=delta.at[c, 1 - core], dst_ref=from_partner.at[c],
            send_sem=p_send, recv_sem=p_recv.at[c],
            device_id={"replica": partner}, device_id_type=MESH,
        )

    def peer_copy(c, step):
        return pltpu.make_async_remote_copy(
            src_ref=pair.at[c, lax.rem(chip + step, chips)], dst_ref=from_peers.at[c, step - 1],
            send_sem=r_send, recv_sem=r_recv.at[c],
            device_id={"replica": peer(step)}, device_id_type=MESH,
        )

    def pair_sum(c):
        partner_copy(c).wait_recv()
        for x in range(chips):
            pair[c, x] = (
                delta[c, core, x].astype(F32) + from_partner[c, x].astype(F32)
            ).astype(BF16)
        for step in range(1, chips):
            peer_copy(c, step).start()

    def spread(c, step):
        piece = na.at[:, chip, core, :, cols(c)]
        return pltpu.make_async_remote_copy(
            src_ref=piece, dst_ref=piece, send_sem=a_send, recv_sem=a_recv.at[c],
            device_id={"replica": peer(step)}, device_id_type=MESH,
        )

    def across(c, side):
        piece = na.at[:, :, side, :, cols(c)]
        return pltpu.make_async_remote_copy(
            src_ref=piece, dst_ref=piece, send_sem=f_send, recv_sem=f_recv,
            device_id={"replica": partner}, device_id_type=MESH,
        )

    def arrived(ref, sem):
        pltpu.make_async_copy(ref, ref, sem).wait()

    def outer(c):
        arrived(from_peers.at[c], r_recv.at[c])
        total = delta[c, core, chip].astype(F32) + from_partner[c, chip].astype(F32)
        for step in range(1, chips):
            total = total + from_peers[c, step - 1].astype(F32)
        average = total / workers
        moved = outer_beta * mom[:, :, cols(c)] + average
        nm[:, :, cols(c)] = moved
        part = anchor[:, r, :, cols(c)].astype(F32)
        na[:, chip, core, :, cols(c)] = (
            part - outer_rate * (average + outer_beta * moved)
        ).astype(BF16)
        for step in range(1, chips):
            spread(c, step).start()

    def pass_on(c):
        arrived(from_peers.at[c], a_recv.at[c])
        across(c, core).start()

    def weigh(c):
        part = pl.ds(pl.multiple_of(c * cw, cw), 2 * cw)
        return dot(
            g[:, :, part].reshape(length, 2 * cw), w[:, :, part].reshape(heads * DH, 2 * cw), 1, 1
        )

    def backward(h):
        hc = head_cols(h)
        kh = k[:, hc]
        ga = gs[:, hc]
        row = jnp.sum(ga.astype(F32) * att[:, hc].astype(F32), axis=-1, keepdims=True)
        gp = dot(ga, v[:, hc], 1, 1)
        s = (probs[h].astype(F32) * (gp - row)).astype(BF16)
        ds[...] = s
        dq[:, hc] = (dot(s, kh, 1, 0) * scale).astype(BF16)
        dv[:, hc] = dot(ga, probs[h], 0, 0).T.astype(BF16)
        dk[:, hc] = (dot(q[:, hc], ds[...], 0, 0) * scale).T.astype(BF16)

    def within(n, count):
        return jnp.logical_and(n >= 0, n < count)

    loads[0].wait()
    first_left()
    for load in loads[1:4]:
        load.wait()
    for h in range(heads):
        if h == min(NEAR_AT, heads - 1):
            first_near()
        if h == min(FAR_AT, heads - 1):
            first_far()
        forward(h)
    for load in loads[4:]:
        load.wait()

    @pl.when(chips - chip - core > 0)
    def _():
        pl.semaphore_wait(side, chips - chip - core)


    behind = jnp.maximum(SKEW_RIGHT * (i - 1) + RIGHT, SKEW * (tensors - 2 - i))
    lag = jnp.where(inner, behind + MID, 0)
    early = jnp.where(inner, 0, EARLY)
    summed = 1 + SUM_LAG
    spreads = summed + SPREAD_LAG

    def order(c):
        return jnp.where(inner, turned(c), c)

    def step(n, carry):
        def go_left(s):
            c = n - SKEW * s

            @pl.when(jnp.logical_and(inner, jnp.logical_and(i + 1 + s < tensors, within(c, CHUNKS))))
            def _():
                relay_left(turned(c), s)

        def go_right(s):
            c = n - RIGHT - SKEW_RIGHT * s

            @pl.when(jnp.logical_and(inner, jnp.logical_and(i - 1 - s >= 0, within(c, CHUNKS))))
            def _():
                relay_right(turned(c), s)

        for s in range(tensors - 1):
            if s == 0 and RIGHT_FIRST:
                go_right(s)
                go_left(s)
            else:
                go_left(s)
                go_right(s)
        later_left(n)
        later_right(n - RIGHT)

        m = n - lag

        @pl.when(jnp.logical_and(jnp.logical_not(inner), m == DIRECT))
        def _():
            if DIRECT > 0:
                pair_sum(DIRECT - 1)
            for c in range(EARLY):
                outer(c)

        @pl.when(within(m, CHUNKS))
        def _():
            @pl.when(jnp.logical_not(inner))
            def _():
                arrive(m)

            adam(order(m))
            partner_copy(order(m)).start()

        @pl.when(m == 2)
        def _():
            gacc[...] = weigh(order(0))

        @pl.when(jnp.logical_and(lax.rem(m + CHUNKS, 2) == 0, jnp.logical_and(m > 2, m < CHUNKS - 2)))
        def _():
            gacc[...] += weigh(order(m - 2))

        @pl.when(m == CHUNKS)
        def _():
            gs[...] = (gacc[...] + weigh(order(CHUNKS - 4)) + weigh(order(CHUNKS - 2))).astype(BF16)

        @pl.when(within(m - CHUNKS - 1, heads))
        def _():
            backward(m - CHUNKS - 1)

        @pl.when(jnp.logical_and(within(m - 1, CHUNKS), jnp.logical_or(inner, m != DIRECT)))
        def _():
            pair_sum(order(m - 1))

        @pl.when(jnp.logical_and(m - summed >= early, m - summed < CHUNKS))
        def _():
            outer(order(m - summed))

        @pl.when(within(m - spreads, CHUNKS))
        def _():
            pass_on(order(m - spreads))

        return carry

    longest = max(SKEW, SKEW_RIGHT) * max(tensors - 3, 0) + RIGHT + MID
    lax.fori_loop(0, longest + CHUNKS + max(spreads, heads + 1), step, 0)
    arrived(from_partner, f_recv)
    drain_gather()
    arrived(from_partner, p_send)
    arrived(from_peers, r_send)
    arrived(from_peers, a_send)
    arrived(from_partner, f_send)


def store(*refs):
    n = (len(refs) - 1) // 2
    copies = [pltpu.make_async_copy(refs[j], refs[n + j], refs[-1].at[j]) for j in range(n)]
    for copy in copies:
        copy.start()
    for copy in copies:
        copy.wait()


def local(tensors, workers, queries, key_rows, value_rows, out_grads, inner_weights, adam_first,
          adam_second, anchor, momentum):
    length, inner = queries.shape[1:]
    rows, width = out_grads.shape[1:]
    heads = inner_weights.shape[1]
    slab = momentum.shape[1]
    chips = workers // 2
    cw = width // CHUNKS
    qs = (length, inner)
    ws = (heads, DH, width)
    an = (heads, workers, slab, width)
    ms = (heads, slab, width)
    S = jax.ShapeDtypeStruct
    hbm = pl.BlockSpec(memory_space=pltpu.HBM)
    V = pltpu.VMEM
    D = pltpu.SemaphoreType.DMA
    nas = (heads, chips, 2, slab, width)
    results = [(qs, BF16)] * 3 + [(ws, BF16)] * 2 + [(nas, BF16), (ms, F32)]
    held = sum(math.prod(shape) * jnp.dtype(dtype).itemsize for shape, dtype in results)
    room = VMEM_BYTES - held - SPARE
    outs = pl.pallas_call(
        functools.partial(kernel, tensors, workers),
        out_shape=[V(shape, dtype) for shape, dtype in results],
        in_specs=[hbm] * 9,
        out_specs=[pl.BlockSpec(memory_space=V)] * 7,
        scratch_shapes=[
            V(qs, BF16), V(qs, BF16), V(qs, BF16), V((tensors, rows, width), BF16),
            V(ws, BF16), V(ws, BF16), V(ws, BF16), V(an, BF16), V(ms, F32),
            V((heads, length, length), BF16), V(qs, BF16), V((heads, DH, length), BF16),
            V((length, length), BF16), V((length, heads * DH), BF16), V((length, heads * DH), F32),
            V((CHUNKS, 2, chips, heads, slab, cw), BF16),
            V((CHUNKS, chips, heads, slab, cw), BF16),
            V((CHUNKS, chips, heads, slab, cw), BF16),
            V((CHUNKS, chips - 1, heads, slab, cw), BF16),
            D((9,)),
            pltpu.SemaphoreType.REGULAR, pltpu.SemaphoreType.REGULAR, pltpu.SemaphoreType.REGULAR,
            D((2, tensors - 1)), D((2,)), D((tensors - 1, CHUNKS)),
            D, D((CHUNKS,)), D, D((CHUNKS,)), D, D((CHUNKS,)), D, D,
        ],
        compiler_params=pltpu.CompilerParams(collective_id=0, has_side_effects=True, vmem_limit_bytes=room),
        name="sync",
    )(
        queries[0], key_rows[0], value_rows[0], out_grads[0], inner_weights[0], adam_first[0],
        adam_second[0], anchor.reshape(an), momentum,
    )
    dq, dk, dv, n1, n2, na, nm = pl.pallas_call(
        store,
        out_shape=[S(shape, dtype) for shape, dtype in results],
        in_specs=[pl.BlockSpec(memory_space=V)] * 7,
        out_specs=[hbm] * 7,
        scratch_shapes=[D((7,))],
        compiler_params=pltpu.CompilerParams(vmem_limit_bytes=2**20),
        name="store",
    )(*outs)
    return dq[None], dk[None], dv[None], n1[None], n2[None], na.reshape(anchor.shape), nm


def solution(mesh):
    workers = P("replica", "tensor", None, None)
    heads = P("replica", None, "tensor")
    specs = (
        heads, heads, heads, P("replica", "tensor", None), workers, workers, workers,
        P("tensor", None, None), P("tensor", "replica", None),
    )
    outs = (
        heads, heads, heads, workers, workers, P("tensor", None, None), P("tensor", "replica", None)
    )
    body = functools.partial(local, mesh.shape["tensor"], mesh.shape["replica"])
    return jax.shard_map(body, mesh=mesh, in_specs=specs, out_specs=outs, check_vma=False)
```
